32 devices in a mesh: gx: 4 (over y, x), gy: 4 (over z), gz: 2 (over core).
Axes of the slice: x: 2, y: 2, z: 4, core: 2. Of those that a mesh axis runs over, the one named last changes fastest.
Arguments:
- particles: float32 [32, 32, 16, 128], P('gx', 'gy', 'gz'), may hold values from -6 to 6, as said below
- counts: int32 [32, 32, 16], P('gx', 'gy', 'gz'), may hold values from 1 to 32, as said below
Outputs:
- potential: float32 [32, 32, 512], P('gx', 'gy', 'gz')
- near_potential: float32 [32, 32, 512], P('gx', 'gy', 'gz')
The draws below stay inside these ranges and needn't reach their ends.
Inputs may be any that keep to these rules, and one draw needn't show every extreme that they name: `particles`: in each leaf the first 96 entries are offsets from the leaf's centre in leaf sides, three blocks of 32 for the three coordinates, within -0.5 and 0.5; the last 32 are strengths. `counts`: slots from the count on are padding; some leaf is full.
All inputs are finite; a program needn't handle non-finite values.
Results may differ from the reference program's by a relative error of at most 0.0003.
Values sent between devices are 32-bit elements; how exact they have to be, the bound alone decides.
A program may use at most 64 MiB of HBM per device.

```python
import math
import jax
import jax.numpy as jnp
from jax import lax

P_SIZE = 32
Q = 64
SIDE = 8
DEPTH = 1
NX = 32
NY = 32
NZ = 16
N_GX = 4
N_GY = 4
N_GZ = 2


def draw_particles(key, part):
    first, second = jax.random.split(jax.random.fold_in(key, 11))
    offsets = jax.random.uniform(first, (NX, NY, NZ, 3 * P_SIZE), jnp.float32, -0.5, 0.5)
    strengths = jnp.clip(jax.random.normal(second, (NX, NY, NZ, P_SIZE), jnp.float32), -6.0, 6.0)
    return jnp.concatenate([offsets, strengths], axis=3)


def draw_counts(key, part):
    first, second, third = jax.random.split(jax.random.fold_in(key, 23), 3)
    values = jax.random.randint(first, (NX, NY, NZ), 1, P_SIZE + 1, dtype=jnp.int32)
    leaves_all = NX * NY * NZ
    chosen_full = jax.random.randint(second, (), 0, leaves_all, dtype=jnp.int32)
    chosen_single = jax.random.randint(third, (), 0, leaves_all, dtype=jnp.int32)
    order = jnp.arange(leaves_all, dtype=jnp.int32).reshape(NX, NY, NZ)
    values = jnp.where(order == chosen_single, 1, values)
    return jnp.where(order == chosen_full, P_SIZE, values)


def setup_inputs(seed: int = 0) -> dict:
    keys = jax.random.split(jax.random.key(seed), 3)
    return {
        "particles": draw_particles(jax.random.fold_in(keys[2], 71), 0),
        "counts": draw_counts(jax.random.fold_in(keys[2], 71), 0),
    }


INV_FOUR_PI = 0.07957747154594767
INNER = 0.9
OUTER = 1.5
PARENT_CHECK = 3.0
SOFTEN_SQUARED = 0.0625
REGULAR = 0.01
HIGHEST = lax.Precision.HIGHEST

def sphere(number):
    order = jnp.arange(number, dtype=jnp.float32)
    height = 1.0 - (2.0 * order + 1.0) / number
    radial = jnp.sqrt(1.0 - height * height)
    turning = order * (math.pi * (3.0 - math.sqrt(5.0)))
    return jnp.stack([radial * jnp.cos(turning), radial * jnp.sin(turning), height])

def green(first, second, third):
    return INV_FOUR_PI / jnp.sqrt(first * first + second * second + third * third)

def factor_lower(normal):
    number = normal.shape[0]
    rows = jnp.arange(number, dtype=jnp.int32)

    def column_turn(column, factor):
        column = column.astype(jnp.int32)
        select = (rows == column).astype(jnp.float32)
        own_row = jnp.dot(select, factor, precision=HIGHEST)
        residue = jnp.dot(normal, select, precision=HIGHEST) - jnp.dot(factor, own_row, precision=HIGHEST)
        pivot = jnp.sqrt(jnp.dot(select, residue, precision=HIGHEST))
        newcol = jnp.where(rows >= column, residue / pivot, 0.0)
        return factor + newcol[:, None] * select[None, :]
    return lax.fori_loop(0, number, column_turn, jnp.zeros_like(normal))

def solve_lower(factor, right):
    number = factor.shape[0]
    rows = jnp.arange(number, dtype=jnp.int32)

    def row_turn(index, result):
        index = index.astype(jnp.int32)
        select = (rows == index).astype(jnp.float32)
        own_row = jnp.dot(select, factor, precision=HIGHEST)
        pivot = jnp.dot(own_row, select, precision=HIGHEST)
        value = (jnp.dot(select, right, precision=HIGHEST) - jnp.dot(own_row, result, precision=HIGHEST)) / pivot
        return result + select[:, None] * value[None, :]
    return lax.fori_loop(0, number, row_turn, jnp.zeros_like(right))

def solve_upper_of(factor, right):
    number = factor.shape[0]
    rows = jnp.arange(number, dtype=jnp.int32)

    def row_turn(step, result):
        index = (number - 1 - step).astype(jnp.int32)
        select = (rows == index).astype(jnp.float32)
        own_row = jnp.dot(factor.T, select, precision=HIGHEST)
        pivot = jnp.dot(own_row, select, precision=HIGHEST)
        value = (jnp.dot(select, right, precision=HIGHEST) - jnp.dot(own_row, result, precision=HIGHEST)) / pivot
        return result + select[:, None] * value[None, :]
    return lax.fori_loop(0, number, row_turn, jnp.zeros_like(right))

def fit_matrix(points):
    number = points.shape[1]
    vectors = OUTER * points[:, :, None] - INNER * points[:, None, :]
    kernel = green(vectors[0], vectors[1], vectors[2])
    normal = jnp.dot(kernel.T, kernel, precision=HIGHEST)
    ridge = REGULAR * jnp.trace(normal) / number
    normal = normal + ridge * jnp.eye(number, dtype=jnp.float32)
    factor = factor_lower(normal)
    middle = solve_lower(factor, kernel.T)
    return solve_upper_of(factor, middle)

def child_table(points, downward):
    half = jnp.array([-0.5, 0.5], dtype=jnp.float32)
    if downward:
        vectors = INNER * points[:, :, None] - PARENT_CHECK * points[:, None, :]
        sign = 1.0
    else:
        vectors = PARENT_CHECK * points[:, :, None] - INNER * points[:, None, :]
        sign = -1.0
    first = vectors[0][None, None, None] + sign * half[:, None, None, None, None]
    second = vectors[1][None, None, None] + sign * half[None, :, None, None, None]
    third = vectors[2][None, None, None] + sign * half[None, None, :, None, None]
    first, second, third = jnp.broadcast_arrays(first, second, third)
    return green(first, second, third)

def multiply_fit(checks, fit):
    return jnp.einsum('...k,jk->...j', checks, fit, precision=HIGHEST)

def apply_down(checks, fit):
    return jnp.einsum('...k,kj->...j', checks, fit, precision=HIGHEST)

def lift(child, up_table, fit):
    a, b, c, q = child.shape
    grouped = child.reshape(a // 2, 2, b // 2, 2, c // 2, 2, q)
    checks = jnp.einsum('axbyczk,xyzjk->abcj', grouped, up_table, precision=HIGHEST)
    return 2.0 * multiply_fit(checks, fit)

def descend(parent, down_table):
    a, b, c, q = parent.shape
    checks = jnp.einsum('abck,xyzjk->axbyczj', parent, down_table, precision=HIGHEST)
    return checks.reshape(2 * a, 2 * b, 2 * c, q)

def split_particles(particles, counts):
    slots = particles.shape[-1] // 4
    positions = particles[..., :3 * slots].reshape(particles.shape[:-1] + (3, slots))
    present = jnp.arange(slots, dtype=jnp.int32) < counts[..., None]
    strengths = jnp.where(present, particles[..., 3 * slots:], 0.0)
    return (positions, strengths)

def upward_checks(positions, strengths, points):
    first = OUTER * points[0][:, None] - positions[..., 0, None, :]
    second = OUTER * points[1][:, None] - positions[..., 1, None, :]
    third = OUTER * points[2][:, None] - positions[..., 2, None, :]
    return lax.optimization_barrier(jnp.sum(green(first, second, third) * strengths[..., None, :], axis=-1))

def local_values(positions, densities, points):
    first = positions[..., 0, :, None] - OUTER * points[0]
    second = positions[..., 1, :, None] - OUTER * points[1]
    third = positions[..., 2, :, None] - OUTER * points[2]
    return lax.optimization_barrier(jnp.sum(green(first, second, third) * densities[..., None, :], axis=-1))

def pair_values(target_positions, source_positions, source_strengths, offset):
    first = target_positions[..., 0, :, None] - source_positions[..., 0, None, :] - offset[0]
    second = target_positions[..., 1, :, None] - source_positions[..., 1, None, :] - offset[1]
    third = target_positions[..., 2, :, None] - source_positions[..., 2, None, :] - offset[2]
    inverse = INV_FOUR_PI / jnp.sqrt(first * first + second * second + third * third + SOFTEN_SQUARED)
    return lax.optimization_barrier(jnp.sum(inverse * source_strengths[..., None, :], axis=-1))

def list_kernels(offsets, points):
    first = INNER * (points[0][:, None] - points[0][None, :]) - offsets[:, 0, None, None]
    second = INNER * (points[1][:, None] - points[1][None, :]) - offsets[:, 1, None, None]
    third = INNER * (points[2][:, None] - points[2][None, :]) - offsets[:, 2, None, None]
    return green(first, second, third)

def far_kernels(delta, points):
    base = INNER * (points[:, :, None] - points[:, None, :])
    first = delta[:, 0, None, None] + base[0]
    second = delta[:, 1, None, None] + base[1]
    third = delta[:, 2, None, None] + base[2]
    spread = lax.optimization_barrier(jnp.max(jnp.abs(delta), axis=1))
    return jnp.where((spread >= 2.0)[:, None, None], green(first, second, third), 0.0)

def allowed(shift, parity):
    return ((shift >= -2 - parity) & (shift <= 3 - parity)).astype(jnp.float32)

def list_level(multipoles, points):
    size_x, size_y, size_z, width = multipoles.shape
    padded = jnp.pad(multipoles, ((3, 3), (3, 3), (3, 3), (0, 0)))
    parity_x = jnp.arange(size_x, dtype=jnp.int32) % 2
    parity_y = jnp.arange(size_y, dtype=jnp.int32) % 2
    parity_z = jnp.arange(size_z, dtype=jnp.int32) % 2

    def list_turn(number, total):
        number = number.astype(jnp.int32)
        shift_x = number // 49
        shift_y = number // 7 % 7
        shift_z = number % 7
        block = lax.dynamic_slice(padded, (shift_x, shift_y, shift_z, jnp.int32(0)), (size_x, size_y, size_z, width))
        offset = jnp.stack([shift_x, shift_y, shift_z]).astype(jnp.float32) - 3.0
        spread = jnp.max(jnp.abs(offset))
        kernel = jnp.where(spread >= 2.0, list_kernels(offset[None, :], points)[0], 0.0)
        weights = allowed(shift_x - 3, parity_x)[:, None, None] * allowed(shift_y - 3, parity_y)[None, :, None] * allowed(shift_z - 3, parity_z)[None, None, :]
        product = jnp.dot(block.reshape(-1, width), kernel.T, precision=HIGHEST).reshape(size_x, size_y, size_z, width)
        return total + weights[..., None] * product
    return lax.fori_loop(0, 343, list_turn, jnp.zeros((size_x, size_y, size_z, width), jnp.float32))

def reference(particles, counts):
    points = sphere(Q)
    fit = fit_matrix(points)
    up_table = child_table(points, False)
    down_table = child_table(points, True)
    positions, strengths = split_particles(particles, counts)
    masked = jnp.concatenate([particles[..., :3 * P_SIZE], strengths], axis=3)
    leaf_checks = lax.map(lambda slab: upward_checks(slab[0], slab[1], points), (positions, strengths))
    leaf_multipoles = jnp.dot(leaf_checks.reshape(-1, Q), fit.T, precision=HIGHEST).reshape(NX, NY, NZ, Q)
    levels = SIDE.bit_length() - 1
    multipoles = [leaf_multipoles]
    for level in range(levels):
        multipoles.append(lift(multipoles[-1], up_table, fit))
    top = multipoles[levels]
    top_z = N_GZ * DEPTH
    top_rows = top.reshape(-1, Q)
    flat = jnp.arange(N_GX * N_GY * top_z, dtype=jnp.int32)
    coords = jnp.stack([flat // (N_GY * top_z), flat // top_z % N_GY, flat % top_z], axis=1).astype(jnp.float32)

    def one_target(target):
        kernels = far_kernels(target[None, :] - coords, points)
        return jnp.einsum('njk,nk->j', kernels, top_rows, precision=HIGHEST)
    far_checks = lax.map(one_target, coords)
    local = apply_down(far_checks, fit).reshape(N_GX, N_GY, top_z, Q)
    for level in range(levels - 1, -1, -1):
        local = apply_down(list_level(multipoles[level], points) + descend(local, down_table), fit)
    leaf_locals = local
    padded_near = jnp.pad(masked, ((1, 1), (1, 1), (1, 1), (0, 0)))

    def row_values(row):
        row = row.astype(jnp.int32)
        row_positions = lax.dynamic_index_in_dim(positions, row, 0, keepdims=False)
        row_locals = lax.dynamic_index_in_dim(leaf_locals, row, 0, keepdims=False)
        far_value = local_values(row_positions, row_locals, points)

        def near_turn(number, total):
            number = number.astype(jnp.int32)
            shift_x = number // 9
            shift_y = number // 3 % 3
            shift_z = number % 3
            block = lax.dynamic_slice(padded_near, (row + shift_x, shift_y, shift_z, jnp.int32(0)), (1, NY, NZ, 4 * P_SIZE))[0]
            source_positions = block[..., :3 * P_SIZE].reshape(NY, NZ, 3, P_SIZE)
            offset = jnp.stack([shift_x, shift_y, shift_z]).astype(jnp.float32) - 1.0
            return total + pair_values(row_positions, source_positions, block[..., 3 * P_SIZE:], offset)
        near_value = lax.fori_loop(0, 27, near_turn, jnp.zeros_like(far_value))
        return (far_value + near_value, near_value)
    values, near_values = lax.map(row_values, jnp.arange(NX, dtype=jnp.int32))
    return (values.reshape(NX, NY, NZ * P_SIZE), near_values.reshape(NX, NY, NZ * P_SIZE))
```

```python
import math

import jax
import jax.numpy as jnp
import ml_dtypes
import numpy as np
from jax import lax
from jax.experimental import pallas as pl
from jax.experimental.pallas import tpu as pltpu
from jax.sharding import PartitionSpec as P

Q = 64
INV_FOUR_PI = 0.07957747154594767
INNER = 0.9
OUTER = 1.5
PARENT_CHECK = 3.0
SOFTEN_SQUARED = 0.0625
REGULAR = 0.01
HIGHEST = lax.Precision.HIGHEST
far_block = 32
AXES = ("gx", "gy", "gz")


def sphere(number):
    order = np.arange(number, dtype=np.float64)
    height = 1.0 - (2.0 * order + 1.0) / number
    radial = np.sqrt(1.0 - height * height)
    turning = order * (math.pi * (3.0 - math.sqrt(5.0)))
    return np.stack([radial * np.cos(turning), radial * np.sin(turning), height])


def green(vectors):
    return INV_FOUR_PI / np.sqrt(np.sum(vectors * vectors, axis=0))


def constant_tables():
    points = sphere(Q)
    kernel = green(OUTER * points[:, :, None] - INNER * points[:, None, :])
    normal = kernel.T @ kernel
    normal = normal + REGULAR * np.trace(normal) / Q * np.eye(Q)
    lower = np.linalg.cholesky(normal)
    fit = np.linalg.solve(lower, kernel.T) / np.diag(lower)[:, None]
    up = np.zeros((8 * Q, Q))
    down = np.zeros((Q, 8 * Q))
    for child in range(8):
        offset = np.array([child // 4, child // 2 % 2, child % 2]) - 0.5
        vectors = PARENT_CHECK * points[:, :, None] - INNER * points[:, None, :]
        upper = green(vectors - offset[:, None, None])
        up[child * Q : (child + 1) * Q] = (2.0 * fit @ upper).T
        vectors = INNER * points[:, :, None] - PARENT_CHECK * points[:, None, :]
        lower = green(vectors + offset[:, None, None])
        down[:, child * Q : (child + 1) * Q] = lower.T @ fit
    base = INNER * (points[:, :, None] - points[:, None, :])
    table = np.zeros((7, 7, 6, Q, 2, Q), np.float32)
    for ox in range(-3, 4):
        for oy in range(-3, 4):
            for sz in range(6):
                for cz in range(2):
                    offset = np.array([ox, oy, sz - 2 - cz], np.float64)
                    if np.max(np.abs(offset)) >= 2:
                        values = green(base - offset[:, None, None])
                        table[ox + 3, oy + 3, sz, :, cz, :] = values.T
    table = table.reshape(7, 7, 6 * Q, 2 * Q)
    high = table.astype(ml_dtypes.bfloat16)
    low = (table - high.astype(np.float32)).astype(ml_dtypes.bfloat16)
    spread = np.repeat((OUTER * points)[:, :, None], 128, axis=2).astype(np.float32)
    pair_fit = np.kron(np.eye(2), fit)
    single = np.float32
    return (
        points.astype(single),
        fit.astype(single),
        up.astype(single),
        down.astype(single),
        high,
        low,
        spread,
        pair_fit.astype(single),
    )


def dot(left, right):
    return jnp.dot(left, right, precision=HIGHEST, preferred_element_type=jnp.float32)


def upward_kernel(part, spread, fit_t, up, leaf, mid, coarse, top, turned):
    for block in range(4):
        turned[...] = part[pl.ds(128 * block, 128), :].T

        def slot_turn(p, total):
            first = spread[0] - turned[pl.ds(p, 1), :]
            second = spread[1] - turned[pl.ds(32 + p, 1), :]
            third = spread[2] - turned[pl.ds(64 + p, 1), :]
            strength = turned[pl.ds(96 + p, 1), :] * INV_FOUR_PI
            inverse = lax.rsqrt(first * first + second * second + third * third)
            return total + inverse * strength

        checks = lax.fori_loop(0, 32, slot_turn, jnp.zeros((Q, 128), jnp.float32))
        leaf[pl.ds(128 * block, 128), :] = dot(checks.T, fit_t[...])
    total = jnp.zeros((64, Q), jnp.float32)
    for child in range(8):
        total = total + dot(leaf[pl.ds(64 * child, 64), :], up[pl.ds(Q * child, Q), :])
    mid[...] = total
    total = jnp.zeros((8, Q), jnp.float32)
    for child in range(8):
        total = total + dot(mid[pl.ds(8 * child, 8), :], up[pl.ds(Q * child, Q), :])
    coarse[...] = total
    row = jnp.zeros((8, Q), jnp.float32)
    for child in range(8):
        own = jnp.broadcast_to(total[child : child + 1], (8, Q))
        row = row + dot(own, up[pl.ds(Q * child, Q), :])
    top[...] = row


def near_kernel(padded, out, rows):
    def pair_turn(pair, carry):
        start = 2 * pair

        def slab(ox, oy, oz):
            return jnp.concatenate(
                [
                    padded[start + ox, pl.ds(oy, 8), oz : oz + 8, :].reshape(64, 128),
                    padded[start + 1 + ox, pl.ds(oy, 8), oz : oz + 8, :].reshape(64, 128),
                ],
                axis=0,
            ).T

        own = slab(1, 1, 1)
        tx, ty, tz = own[0:32], own[32:64], own[64:96]
        square = tx * tx + ty * ty + tz * tz + SOFTEN_SQUARED

        def offset_turn(number, total):
            ox = number // 3
            oy = number % 3
            for oz in range(3):
                source = slab(ox, oy, oz)
                sx = source[0:32] + (ox - 1).astype(jnp.float32)
                sy = source[32:64] + (oy - 1).astype(jnp.float32)
                sz = source[64:96] + (oz - 1.0)
                rows[0:32] = -2.0 * sx
                rows[32:64] = -2.0 * sy
                rows[64:96] = -2.0 * sz
                rows[96:128] = sx * sx + sy * sy + sz * sz
                rows[128:160] = source[96:128] * INV_FOUR_PI

                def source_turn(p, total):
                    distance = (square + rows[pl.ds(96 + p, 1), :]) + (
                        tx * rows[pl.ds(p, 1), :]
                        + ty * rows[pl.ds(32 + p, 1), :]
                        + tz * rows[pl.ds(64 + p, 1), :]
                    )
                    return total + lax.rsqrt(distance) * rows[pl.ds(128 + p, 1), :]

                total = lax.fori_loop(0, 32, source_turn, total, unroll=8)
            return total

        total = lax.fori_loop(0, 9, offset_turn, jnp.zeros((32, 128), jnp.float32))
        out[pl.ds(pl.multiple_of(128 * pair, 128), 128), :] = total.T
        return carry

    lax.fori_loop(0, 4, pair_turn, 0)


def downward_kernel(
    windows, small, high, low, pair_fit, down, top_local, part, spread, out, total, turned, local
):
    total[...] = jnp.zeros_like(total)

    def source_turn(number, carry):
        sx = number // 6
        sy = number % 6
        pieces = []
        for cx in range(2):
            for cy in range(2):
                for cz in range(2):
                    pieces.append(windows[sx + 2 * cx, sy + 2 * cy, pl.ds(8 * cz, 8), :])
        pieces.append(small[sx, sy])
        left = jnp.concatenate(pieces, axis=0)
        left_high = left.astype(jnp.bfloat16)
        left_low = (left - left_high.astype(jnp.float32)).astype(jnp.bfloat16)
        both = jnp.concatenate([left_high, left_low], axis=0)
        places = [(sx + 1 - cx, sy + 1 - cy) for cx in range(2) for cy in range(2)]
        right_high = jnp.concatenate([high[a, b] for a, b in places], axis=1)
        right_low = jnp.concatenate([low[a, b] for a, b in places], axis=1)
        first = jnp.dot(both, right_high, preferred_element_type=jnp.float32)
        second = jnp.dot(left_high, right_low, preferred_element_type=jnp.float32)
        total[...] += first[:80] + first[80:] + second
        return carry

    lax.fori_loop(0, 36, source_turn, 0)
    fitted = jnp.concatenate(
        [dot(total[:, 128 * pair : 128 * pair + 128], pair_fit[...]) for pair in range(4)], axis=1
    )

    def regroup(rows):
        return jnp.concatenate([rows[:, Q * c : Q * c + Q] for c in range(8)], axis=0)

    coarse = fitted[72:80] + dot(top_local[...], down[...])
    coarse = regroup(coarse[0:1])
    mid = regroup(fitted[64:72] + dot(coarse, down[...]))
    leaf = fitted[0:64] + dot(mid, down[...])
    for block in range(4):
        turned[...] = part[pl.ds(128 * block, 128), :].T
        own = leaf[:, 128 * block : 128 * block + 128]
        own = jnp.concatenate([own[:, :Q], own[:, Q:]], axis=0)
        local[...] = own.T * INV_FOUR_PI
        tx, ty, tz = turned[0:32], turned[32:64], turned[64:96]

        def point_turn(k, value):
            first = tx - spread[0, pl.ds(k, 1), :]
            second = ty - spread[1, pl.ds(k, 1), :]
            third = tz - spread[2, pl.ds(k, 1), :]
            inverse = lax.rsqrt(first * first + second * second + third * third)
            return value + inverse * local[pl.ds(k, 1), :]

        value = lax.fori_loop(0, Q, point_turn, jnp.zeros((32, 128), jnp.float32), unroll=4)
        out[pl.ds(128 * block, 128), :] = value.T


def run(kernel, outs, scratch, cost, *args):
    return pl.pallas_call(
        kernel,
        out_shape=outs,
        scratch_shapes=[pltpu.VMEM(shape, jnp.float32) for shape in scratch],
        compiler_params=pltpu.CompilerParams(vmem_limit_bytes=40 << 20),
        cost_estimate=pl.CostEstimate(flops=cost, bytes_accessed=1 << 20, transcendentals=0),
    )(*args)


def single(*shape):
    return jax.ShapeDtypeStruct(shape, jnp.float32)


def nested(cells):
    split = cells.reshape((2,) * 9 + cells.shape[3:])
    return split.transpose(2, 5, 8, 1, 4, 7, 0, 3, 6, 9).reshape(512, -1)


def plain(rows):
    split = rows.reshape((2,) * 9 + rows.shape[1:])
    return split.transpose(6, 3, 0, 7, 4, 1, 8, 5, 2, 9).reshape(8, 8, 8, -1)


def plain_mid(rows):
    split = rows.reshape((2,) * 6 + rows.shape[1:])
    return split.transpose(3, 0, 4, 1, 5, 2, 6).reshape(4, 4, 4, -1)


def extended(arrays, width):
    for axis, dim in (("gz", 2), ("gy", 1), ("gx", 0)):
        count = lax.axis_size(axis)
        heads = [lax.slice_in_dim(a, 0, width, axis=dim) for a in arrays]
        tails = [lax.slice_in_dim(a, a.shape[dim] - width, a.shape[dim], axis=dim) for a in arrays]
        forward = [(i, i + 1) for i in range(count - 1)]
        backward = [(i + 1, i) for i in range(count - 1)]

        def pack(parts):
            return jnp.concatenate([x.reshape(-1, x.shape[-1]) for x in parts], axis=0)

        def unpack(rows, parts):
            result, start = [], 0
            for x in parts:
                length = x.size // x.shape[-1]
                result.append(rows[start : start + length].reshape(x.shape))
                start += length
            return result

        before = unpack(lax.ppermute(pack(tails), axis, forward), tails)
        after = unpack(lax.ppermute(pack(heads), axis, backward), heads)
        arrays = [
            jnp.concatenate([b, a, c], axis=dim) for b, a, c in zip(before, arrays, after)
        ]
    return arrays


def far_local(top_row, points, fit):
    grid_y = lax.axis_size("gy")
    grid_z = lax.axis_size("gz")
    devices = lax.axis_size("gx") * grid_y * grid_z
    gathered = lax.all_gather(top_row, AXES, axis=0, tiled=True)
    own = jnp.stack([lax.axis_index(axis) for axis in AXES]).astype(jnp.float32)
    base = INNER * (points[:, :, None] - points[:, None, :])

    def block_term(total, number):
        rows = lax.dynamic_slice_in_dim(gathered, number * far_block, far_block, 0)
        flat = number * far_block + jnp.arange(far_block, dtype=jnp.int32)
        boxes = jnp.stack(
            [flat // (grid_y * grid_z), flat // grid_z % grid_y, flat % grid_z], axis=1
        )
        delta = own[None, :] - boxes.astype(jnp.float32)
        spread = jnp.max(jnp.abs(delta), axis=1)
        first = delta[:, 0, None, None] + base[0]
        second = delta[:, 1, None, None] + base[1]
        third = delta[:, 2, None, None] + base[2]
        square = first * first + second * second + third * third
        kernels = jnp.where(
            (spread >= 2.0)[:, None, None], INV_FOUR_PI / jnp.sqrt(square), 0.0
        )
        return (total + jnp.sum(kernels * rows[:, None, :], axis=(0, 2)), None)

    blocks = devices // far_block
    check, _ = lax.scan(
        block_term, jnp.zeros((Q,), jnp.float32), jnp.arange(blocks, dtype=jnp.int32)
    )
    return jnp.dot(check[None, :], fit, precision=HIGHEST)


def per_device(particles, counts):
    points, fit, up, down, high, low, spread, pair_fit = constant_tables()
    slots = particles.shape[3] // 4
    present = jnp.arange(slots, dtype=jnp.int32) < counts[..., None]
    masked = jnp.concatenate(
        [particles[..., : 3 * slots], jnp.where(present, particles[..., 3 * slots :], 0.0)], axis=3
    )
    part = nested(masked)
    leaf, mid, coarse, top = run(
        upward_kernel,
        (single(512, Q), single(64, Q), single(8, Q), single(8, Q)),
        [(128, 128)],
        1 << 30,
        part,
        spread,
        np.ascontiguousarray(fit.T),
        up,
    )
    (padded_near,) = extended([masked], 1)
    near = run(near_kernel, single(512, 32), [(160, 128)], 30 << 30, padded_near)
    top_local = far_local(top[0:1], points, fit)
    leaf_cells, mid_cells, coarse_cells = extended(
        [plain(leaf), plain_mid(mid), coarse.reshape(2, 2, 2, Q)], 2
    )
    leaf_cells = leaf_cells.reshape(12, 12, 12 * Q)
    windows = jnp.stack(
        [
            leaf_cells[4 * gx : 4 * gx + 8, 4 * gy : 4 * gy + 8, Q * start : Q * start + 6 * Q]
            for cz in range(2)
            for gx in range(2)
            for gy in range(2)
            for start in (2 * cz, 4 + 2 * cz)
        ],
        axis=2,
    )
    mid_cells = mid_cells.reshape(8, 8, 8 * Q)
    small = jnp.stack(
        [
            mid_cells[2 * gx : 2 * gx + 6, 2 * gy : 2 * gy + 6, 2 * gz * Q : (2 * gz + 6) * Q]
            for gx in range(2)
            for gy in range(2)
            for gz in range(2)
        ]
        + [coarse_cells.reshape(6, 6, 6 * Q)]
        + [jnp.zeros((6, 6, 6 * Q), jnp.float32)] * 7,
        axis=2,
    )
    far = run(
        downward_kernel,
        single(512, 32),
        [(80, 512), (128, 128), (Q, 128)],
        8 << 30,
        windows,
        small,
        high,
        low,
        pair_fit,
        down,
        jnp.broadcast_to(top_local, (8, Q)),
        part,
        spread,
    )
    near = near.reshape(8, 8, 8 * slots)
    return (plain(far).reshape(8, 8, 8 * slots) + near, near)


def solution(mesh):
    placed = (P("gx", "gy", "gz", None), P("gx", "gy", "gz"))
    return jax.shard_map(
        per_device,
        mesh=mesh,
        in_specs=placed,
        out_specs=(P("gx", "gy", "gz"), P("gx", "gy", "gz")),
        check_vma=False,
    )
```

```python
import functools
import math

import jax
import jax.numpy as jnp
import ml_dtypes
import numpy as np
from jax import lax
from jax.experimental import pallas as pl
from jax.experimental.pallas import tpu as pltpu
from jax.sharding import PartitionSpec as P

Q = 64
INV_FOUR_PI = 0.07957747154594767
INNER = 0.9
OUTER = 1.5
PARENT_CHECK = 3.0
SOFTEN_SQUARED = 0.0625
REGULAR = 0.01
HIGHEST = lax.Precision.HIGHEST
far_block = 32
AXES = ("gx", "gy", "gz")


def sphere(number):
    order = np.arange(number, dtype=np.float64)
    height = 1.0 - (2.0 * order + 1.0) / number
    radial = np.sqrt(1.0 - height * height)
    turning = order * (math.pi * (3.0 - math.sqrt(5.0)))
    return np.stack([radial * np.cos(turning), radial * np.sin(turning), height])


def green(vectors):
    return INV_FOUR_PI / np.sqrt(np.sum(vectors * vectors, axis=0))


def constant_tables():
    points = sphere(Q)
    kernel = green(OUTER * points[:, :, None] - INNER * points[:, None, :])
    normal = kernel.T @ kernel
    normal = normal + REGULAR * np.trace(normal) / Q * np.eye(Q)
    lower = np.linalg.cholesky(normal)
    fit = np.linalg.solve(lower, kernel.T) / np.diag(lower)[:, None]
    up = np.zeros((8 * Q, Q))
    down = np.zeros((Q, 8 * Q))
    for child in range(8):
        offset = np.array([child // 4, child // 2 % 2, child % 2]) - 0.5
        vectors = PARENT_CHECK * points[:, :, None] - INNER * points[:, None, :]
        upper = green(vectors - offset[:, None, None])
        up[child * Q : (child + 1) * Q] = (2.0 * fit @ upper).T
        vectors = INNER * points[:, :, None] - PARENT_CHECK * points[:, None, :]
        lower = green(vectors + offset[:, None, None])
        down[:, child * Q : (child + 1) * Q] = lower.T @ fit
    base = INNER * (points[:, :, None] - points[:, None, :])
    table = np.zeros((7, 7, 6, Q, 2, Q), np.float32)
    for ox in range(-3, 4):
        for oy in range(-3, 4):
            for sz in range(6):
                for cz in range(2):
                    offset = np.array([ox, oy, sz - 2 - cz], np.float64)
                    if np.max(np.abs(offset)) >= 2:
                        values = green(base - offset[:, None, None])
                        table[ox + 3, oy + 3, sz, :, cz, :] = values.T
    table = table.reshape(7, 7, 6 * Q, 2 * Q)
    high = table.astype(ml_dtypes.bfloat16)
    low = (table - high.astype(np.float32)).astype(ml_dtypes.bfloat16)
    spread = np.repeat((OUTER * points)[:, :, None], 128, axis=2).astype(np.float32)
    pair_fit = np.kron(np.eye(2), fit)
    single = np.float32
    return (
        points.astype(single),
        fit.astype(single),
        up.astype(single),
        down.astype(single),
        high,
        low,
        spread,
        pair_fit.astype(single),
    )


def dot(left, right):
    return jnp.dot(left, right, precision=HIGHEST, preferred_element_type=jnp.float32)


def upward_kernel(part, spread, fit_t, up, leaf, mid, coarse, top, turned):
    for block in range(4):
        turned[...] = part[pl.ds(128 * block, 128), :].T

        def slot_turn(p, total):
            first = spread[0] - turned[pl.ds(p, 1), :]
            second = spread[1] - turned[pl.ds(32 + p, 1), :]
            third = spread[2] - turned[pl.ds(64 + p, 1), :]
            strength = turned[pl.ds(96 + p, 1), :] * INV_FOUR_PI
            inverse = lax.rsqrt(first * first + second * second + third * third)
            return total + inverse * strength

        checks = lax.fori_loop(0, 32, slot_turn, jnp.zeros((Q, 128), jnp.float32))
        leaf[pl.ds(128 * block, 128), :] = dot(checks.T, fit_t[...])
    total = jnp.zeros((64, Q), jnp.float32)
    for child in range(8):
        total = total + dot(leaf[pl.ds(64 * child, 64), :], up[pl.ds(Q * child, Q), :])
    mid[...] = total
    total = jnp.zeros((8, Q), jnp.float32)
    for child in range(8):
        total = total + dot(mid[pl.ds(8 * child, 8), :], up[pl.ds(Q * child, Q), :])
    coarse[...] = total
    row = jnp.zeros((8, Q), jnp.float32)
    for child in range(8):
        own = jnp.broadcast_to(total[child : child + 1], (8, Q))
        row = row + dot(own, up[pl.ds(Q * child, Q), :])
    top[...] = row


def near_kernel(start, padded, out, rows):

    def slab(ox, oy, oz):
        return jnp.concatenate(
            [
                padded[start + ox, pl.ds(oy, 8), oz : oz + 8, :].reshape(64, 128),
                padded[start + 1 + ox, pl.ds(oy, 8), oz : oz + 8, :].reshape(64, 128),
            ],
            axis=0,
        ).T

    own = slab(1, 1, 1)
    tx, ty, tz = own[0:32], own[32:64], own[64:96]
    square = tx * tx + ty * ty + tz * tz + SOFTEN_SQUARED

    def offset_turn(number, total):
        ox = number // 3
        oy = number % 3
        for oz in range(3):
            source = slab(ox, oy, oz)
            sx = source[0:32] + (ox - 1).astype(jnp.float32)
            sy = source[32:64] + (oy - 1).astype(jnp.float32)
            sz = source[64:96] + (oz - 1.0)
            rows[0:32] = -2.0 * sx
            rows[32:64] = -2.0 * sy
            rows[64:96] = -2.0 * sz
            rows[96:128] = sx * sx + sy * sy + sz * sz
            rows[128:160] = source[96:128] * INV_FOUR_PI

            def source_turn(p, total):
                distance = (square + rows[pl.ds(96 + p, 1), :]) + (
                    tx * rows[pl.ds(p, 1), :]
                    + ty * rows[pl.ds(32 + p, 1), :]
                    + tz * rows[pl.ds(64 + p, 1), :]
                )
                return total + lax.rsqrt(distance) * rows[pl.ds(128 + p, 1), :]

            total = lax.fori_loop(0, 32, source_turn, total, unroll=8)
        return total

    total = lax.fori_loop(0, 9, offset_turn, jnp.zeros((32, 128), jnp.float32))
    out[...] = total.T


def downward_kernel(
    windows, small, high, low, pair_fit, down, top_local, part, spread, out, total, turned, local
):
    total[...] = jnp.zeros_like(total)

    def source_turn(number, carry):
        sx = number // 6
        sy = number % 6
        pieces = []
        for cx in range(2):
            for cy in range(2):
                for cz in range(2):
                    pieces.append(windows[sx + 2 * cx, sy + 2 * cy, pl.ds(8 * cz, 8), :])
        pieces.append(small[sx, sy])
        left = jnp.concatenate(pieces, axis=0)
        left_high = left.astype(jnp.bfloat16)
        left_low = (left - left_high.astype(jnp.float32)).astype(jnp.bfloat16)
        both = jnp.concatenate([left_high, left_low], axis=0)
        places = [(sx + 1 - cx, sy + 1 - cy) for cx in range(2) for cy in range(2)]
        right_high = jnp.concatenate([high[a, b] for a, b in places], axis=1)
        right_low = jnp.concatenate([low[a, b] for a, b in places], axis=1)
        first = jnp.dot(both, right_high, preferred_element_type=jnp.float32)
        second = jnp.dot(left_high, right_low, preferred_element_type=jnp.float32)
        total[...] += first[:80] + first[80:] + second
        return carry

    lax.fori_loop(0, 36, source_turn, 0)
    fitted = jnp.concatenate(
        [dot(total[:, 128 * pair : 128 * pair + 128], pair_fit[...]) for pair in range(4)], axis=1
    )

    def regroup(rows):
        return jnp.concatenate([rows[:, Q * c : Q * c + Q] for c in range(8)], axis=0)

    coarse = fitted[72:80] + dot(top_local[...], down[...])
    coarse = regroup(coarse[0:1])
    mid = regroup(fitted[64:72] + dot(coarse, down[...]))
    leaf = fitted[0:64] + dot(mid, down[...])
    for block in range(4):
        turned[...] = part[pl.ds(128 * block, 128), :].T
        own = leaf[:, 128 * block : 128 * block + 128]
        own = jnp.concatenate([own[:, :Q], own[:, Q:]], axis=0)
        local[...] = own.T * INV_FOUR_PI
        tx, ty, tz = turned[0:32], turned[32:64], turned[64:96]

        def point_turn(k, value):
            first = tx - spread[0, pl.ds(k, 1), :]
            second = ty - spread[1, pl.ds(k, 1), :]
            third = tz - spread[2, pl.ds(k, 1), :]
            inverse = lax.rsqrt(first * first + second * second + third * third)
            return value + inverse * local[pl.ds(k, 1), :]

        value = lax.fori_loop(0, Q, point_turn, jnp.zeros((32, 128), jnp.float32), unroll=4)
        out[pl.ds(128 * block, 128), :] = value.T


def run(kernel, outs, scratch, cost, *args):
    return pl.pallas_call(
        kernel,
        out_shape=outs,
        scratch_shapes=[pltpu.VMEM(shape, jnp.float32) for shape in scratch],
        compiler_params=pltpu.CompilerParams(vmem_limit_bytes=40 << 20),
        cost_estimate=pl.CostEstimate(flops=cost, bytes_accessed=1 << 20, transcendentals=0),
    )(*args)


def single(*shape):
    return jax.ShapeDtypeStruct(shape, jnp.float32)


def nested(cells):
    split = cells.reshape((2,) * 9 + cells.shape[3:])
    return split.transpose(2, 5, 8, 1, 4, 7, 0, 3, 6, 9).reshape(512, -1)


def plain(rows):
    split = rows.reshape((2,) * 9 + rows.shape[1:])
    return split.transpose(6, 3, 0, 7, 4, 1, 8, 5, 2, 9).reshape(8, 8, 8, -1)


def plain_mid(rows):
    split = rows.reshape((2,) * 6 + rows.shape[1:])
    return split.transpose(3, 0, 4, 1, 5, 2, 6).reshape(4, 4, 4, -1)


def extended(arrays, width):
    for axis, dim in (("gz", 2), ("gy", 1), ("gx", 0)):
        count = lax.axis_size(axis)
        heads = [lax.slice_in_dim(a, 0, width, axis=dim) for a in arrays]
        tails = [lax.slice_in_dim(a, a.shape[dim] - width, a.shape[dim], axis=dim) for a in arrays]
        forward = [(i, i + 1) for i in range(count - 1)]
        backward = [(i + 1, i) for i in range(count - 1)]

        def pack(parts):
            return jnp.concatenate([x.reshape(-1, x.shape[-1]) for x in parts], axis=0)

        def unpack(rows, parts):
            result, start = [], 0
            for x in parts:
                length = x.size // x.shape[-1]
                result.append(rows[start : start + length].reshape(x.shape))
                start += length
            return result

        before = unpack(lax.ppermute(pack(tails), axis, forward), tails)
        after = unpack(lax.ppermute(pack(heads), axis, backward), heads)
        arrays = [
            jnp.concatenate([b, a, c], axis=dim) for b, a, c in zip(before, arrays, after)
        ]
    return arrays


def far_local(top_row, points, fit):
    gathered = top_row
    index = jnp.zeros((1, 3), jnp.int32) + jnp.stack([lax.axis_index(axis) for axis in AXES])
    for place, axis in ((2, "gz"), (1, "gy"), (0, "gx")):
        count = lax.axis_size(axis)
        step, length = 1, gathered.shape[0]
        while step < count:
            take = min(step, count - step) * length
            ring = [(i, (i + step) % count) for i in range(count)]
            arrived = lax.ppermute(gathered[:take], axis, ring)
            from_index = index[:take, place] + (count - step)
            from_index = jnp.where(from_index >= count, from_index - count, from_index)
            moved = index[:take].at[:, place].set(from_index)
            gathered = jnp.concatenate([gathered, arrived], axis=0)
            index = jnp.concatenate([index, moved], axis=0)
            step *= 2
    own = jnp.stack([lax.axis_index(axis) for axis in AXES]).astype(jnp.float32)
    base = INNER * (points[:, :, None] - points[:, None, :])

    def block_term(total, number):
        rows = lax.dynamic_slice_in_dim(gathered, number * far_block, far_block, 0)
        boxes = lax.dynamic_slice_in_dim(index, number * far_block, far_block, 0)
        delta = own[None, :] - boxes.astype(jnp.float32)
        spread = jnp.max(jnp.abs(delta), axis=1)
        first = delta[:, 0, None, None] + base[0]
        second = delta[:, 1, None, None] + base[1]
        third = delta[:, 2, None, None] + base[2]
        square = first * first + second * second + third * third
        kernels = jnp.where(
            (spread >= 2.0)[:, None, None], INV_FOUR_PI / jnp.sqrt(square), 0.0
        )
        return (total + jnp.sum(kernels * rows[:, None, :], axis=(0, 2)), None)

    blocks = gathered.shape[0] // far_block
    check, _ = lax.scan(
        block_term, jnp.zeros((Q,), jnp.float32), jnp.arange(blocks, dtype=jnp.int32)
    )
    return jnp.dot(check[None, :], fit, precision=HIGHEST)


def per_device(particles, counts):
    points, fit, up, down, high, low, spread, pair_fit = constant_tables()
    slots = particles.shape[3] // 4
    present = jnp.arange(slots, dtype=jnp.int32) < counts[..., None]
    masked = jnp.concatenate(
        [particles[..., : 3 * slots], jnp.where(present, particles[..., 3 * slots :], 0.0)], axis=3
    )
    part = nested(masked)
    leaf, mid, coarse, top = run(
        upward_kernel,
        (single(512, Q), single(64, Q), single(8, Q), single(8, Q)),
        [(128, 128)],
        1 << 30,
        part,
        spread,
        np.ascontiguousarray(fit.T),
        up,
    )
    (padded_near,) = extended([masked], 1)
    near = jnp.concatenate(
        [
            run(
                functools.partial(near_kernel, start),
                single(128, 32),
                [(160, 128)],
                8 << 30,
                padded_near,
            )
            for start in (0, 2, 4, 6)
        ],
        axis=0,
    )
    top_local = far_local(top[0:1], points, fit)
    leaf_cells, mid_cells, coarse_cells = extended(
        [plain(leaf), plain_mid(mid), coarse.reshape(2, 2, 2, Q)], 2
    )
    leaf_cells = leaf_cells.reshape(12, 12, 12 * Q)
    windows = jnp.stack(
        [
            leaf_cells[4 * gx : 4 * gx + 8, 4 * gy : 4 * gy + 8, Q * start : Q * start + 6 * Q]
            for cz in range(2)
            for gx in range(2)
            for gy in range(2)
            for start in (2 * cz, 4 + 2 * cz)
        ],
        axis=2,
    )
    mid_cells = mid_cells.reshape(8, 8, 8 * Q)
    small = jnp.stack(
        [
            mid_cells[2 * gx : 2 * gx + 6, 2 * gy : 2 * gy + 6, 2 * gz * Q : (2 * gz + 6) * Q]
            for gx in range(2)
            for gy in range(2)
            for gz in range(2)
        ]
        + [coarse_cells.reshape(6, 6, 6 * Q)]
        + [jnp.zeros((6, 6, 6 * Q), jnp.float32)] * 7,
        axis=2,
    )
    far = run(
        downward_kernel,
        single(512, 32),
        [(80, 512), (128, 128), (Q, 128)],
        8 << 30,
        windows,
        small,
        high,
        low,
        pair_fit,
        down,
        jnp.broadcast_to(top_local, (8, Q)),
        part,
        spread,
    )
    near = near.reshape(8, 8, 8 * slots)
    return (plain(far).reshape(8, 8, 8 * slots) + near, near)


def solution(mesh):
    placed = (P("gx", "gy", "gz", None), P("gx", "gy", "gz"))
    return jax.shard_map(
        per_device,
        mesh=mesh,
        in_specs=placed,
        out_specs=(P("gx", "gy", "gz"), P("gx", "gy", "gz")),
        check_vma=False,
    )
```

```python
import functools
import math

import jax
import jax.numpy as jnp
import ml_dtypes
import numpy as np
from jax import lax
from jax.experimental import pallas as pl
from jax.experimental.pallas import tpu as pltpu
from jax.sharding import PartitionSpec as P

Q = 64
INV_FOUR_PI = 0.07957747154594767
INNER = 0.9
OUTER = 1.5
PARENT_CHECK = 3.0
SOFTEN_SQUARED = 0.0625
REGULAR = 0.01
HIGHEST = lax.Precision.HIGHEST
far_block = 32
AXES = ("gx", "gy", "gz")


def sphere(number):
    order = np.arange(number, dtype=np.float64)
    height = 1.0 - (2.0 * order + 1.0) / number
    radial = np.sqrt(1.0 - height * height)
    turning = order * (math.pi * (3.0 - math.sqrt(5.0)))
    return np.stack([radial * np.cos(turning), radial * np.sin(turning), height])


def green(vectors):
    return INV_FOUR_PI / np.sqrt(np.sum(vectors * vectors, axis=0))


def constant_tables():
    points = sphere(Q)
    kernel = green(OUTER * points[:, :, None] - INNER * points[:, None, :])
    normal = kernel.T @ kernel
    normal = normal + REGULAR * np.trace(normal) / Q * np.eye(Q)
    lower = np.linalg.cholesky(normal)
    fit = np.linalg.solve(lower, kernel.T) / np.diag(lower)[:, None]
    up = np.zeros((8 * Q, Q))
    down = np.zeros((Q, 8 * Q))
    for child in range(8):
        offset = np.array([child // 4, child // 2 % 2, child % 2]) - 0.5
        vectors = PARENT_CHECK * points[:, :, None] - INNER * points[:, None, :]
        upper = green(vectors - offset[:, None, None])
        up[child * Q : (child + 1) * Q] = (2.0 * fit @ upper).T
        vectors = INNER * points[:, :, None] - PARENT_CHECK * points[:, None, :]
        lower = green(vectors + offset[:, None, None])
        down[:, child * Q : (child + 1) * Q] = lower.T @ fit
    base = INNER * (points[:, :, None] - points[:, None, :])
    table = np.zeros((7, 7, 6, Q, 2, Q), np.float32)
    for ox in range(-3, 4):
        for oy in range(-3, 4):
            for sz in range(6):
                for cz in range(2):
                    offset = np.array([ox, oy, sz - 2 - cz], np.float64)
                    if np.max(np.abs(offset)) >= 2:
                        values = green(base - offset[:, None, None])
                        table[ox + 3, oy + 3, sz, :, cz, :] = values.T
    table = table.reshape(7, 7, 6 * Q, 2 * Q)
    high = table.astype(ml_dtypes.bfloat16)
    low = (table - high.astype(np.float32)).astype(ml_dtypes.bfloat16)
    spread = np.repeat((OUTER * points)[:, :, None], 128, axis=2).astype(np.float32)
    pair_fit = np.kron(np.eye(2), fit)
    single = np.float32
    return (
        points.astype(single),
        fit.astype(single),
        up.astype(single),
        down.astype(single),
        high,
        low,
        spread,
        pair_fit.astype(single),
    )


def dot(left, right):
    return jnp.dot(left, right, precision=HIGHEST, preferred_element_type=jnp.float32)


def upward_kernel(part, spread, fit_t, up, leaf, mid, coarse, top, turned):
    for block in range(4):
        turned[...] = part[pl.ds(128 * block, 128), :].T

        def slot_turn(p, total):
            first = spread[0] - turned[pl.ds(p, 1), :]
            second = spread[1] - turned[pl.ds(32 + p, 1), :]
            third = spread[2] - turned[pl.ds(64 + p, 1), :]
            strength = turned[pl.ds(96 + p, 1), :] * INV_FOUR_PI
            inverse = lax.rsqrt(first * first + second * second + third * third)
            return total + inverse * strength

        checks = lax.fori_loop(0, 32, slot_turn, jnp.zeros((Q, 128), jnp.float32))
        leaf[pl.ds(128 * block, 128), :] = dot(checks.T, fit_t[...])
    total = jnp.zeros((64, Q), jnp.float32)
    for child in range(8):
        total = total + dot(leaf[pl.ds(64 * child, 64), :], up[pl.ds(Q * child, Q), :])
    mid[...] = total
    total = jnp.zeros((8, Q), jnp.float32)
    for child in range(8):
        total = total + dot(mid[pl.ds(8 * child, 8), :], up[pl.ds(Q * child, Q), :])
    coarse[...] = total
    row = jnp.zeros((8, Q), jnp.float32)
    for child in range(8):
        own = jnp.broadcast_to(total[child : child + 1], (8, Q))
        row = row + dot(own, up[pl.ds(Q * child, Q), :])
    top[...] = row


def near_kernel(start, padded, out, rows):

    def slab(ox, oy, oz):
        return jnp.concatenate(
            [
                padded[start + ox, pl.ds(oy, 8), oz : oz + 8, :].reshape(64, 128),
                padded[start + 1 + ox, pl.ds(oy, 8), oz : oz + 8, :].reshape(64, 128),
            ],
            axis=0,
        ).T

    own = slab(1, 1, 1)
    tx, ty, tz = own[0:32], own[32:64], own[64:96]
    square = tx * tx + ty * ty + tz * tz + SOFTEN_SQUARED

    def offset_turn(number, total):
        ox = number // 3
        oy = number % 3
        for oz in range(3):
            source = slab(ox, oy, oz)
            sx = source[0:32] + (ox - 1).astype(jnp.float32)
            sy = source[32:64] + (oy - 1).astype(jnp.float32)
            sz = source[64:96] + (oz - 1.0)
            rows[0:32] = -2.0 * sx
            rows[32:64] = -2.0 * sy
            rows[64:96] = -2.0 * sz
            rows[96:128] = sx * sx + sy * sy + sz * sz
            rows[128:160] = source[96:128] * INV_FOUR_PI

            def source_turn(p, total):
                distance = (square + rows[pl.ds(96 + p, 1), :]) + (
                    tx * rows[pl.ds(p, 1), :]
                    + ty * rows[pl.ds(32 + p, 1), :]
                    + tz * rows[pl.ds(64 + p, 1), :]
                )
                return total + lax.rsqrt(distance) * rows[pl.ds(128 + p, 1), :]

            total = lax.fori_loop(0, 32, source_turn, total, unroll=8)
        return total

    total = lax.fori_loop(0, 9, offset_turn, jnp.zeros((32, 128), jnp.float32))
    out[...] = total.T


def downward_kernel(
    leaf_cells,
    mid_cells,
    coarse_cells,
    high,
    low,
    pair_fit,
    down,
    top_local,
    part,
    spread,
    out,
    total,
    turned,
    local,
    windows,
    small,
):
    total[...] = jnp.zeros_like(total)

    def window_turn(number, carry):
        ux = number // 8
        uy = number % 8
        row = 0
        for cz in range(2):
            for gx in range(2):
                for gy in range(2):
                    line = leaf_cells[pl.ds((ux + 4 * gx) * 12 + uy + 4 * gy, 1), :]
                    for start in (2 * cz * Q, (4 + 2 * cz) * Q):
                        windows[ux, uy, row : row + 1, :] = line[:, start : start + 6 * Q]
                        row += 1
        return carry

    lax.fori_loop(0, 64, window_turn, 0)

    def small_turn(number, carry):
        sx = number // 6
        sy = number % 6
        row = 0
        for gx in range(2):
            for gy in range(2):
                line = mid_cells[pl.ds((sx + 2 * gx) * 8 + sy + 2 * gy, 1), :]
                for start in (0, 2 * Q):
                    small[sx, sy, row : row + 1, :] = line[:, start : start + 6 * Q]
                    row += 1
        own = coarse_cells[pl.ds(number, 1), :]
        small[sx, sy, 8:16, :] = jnp.broadcast_to(own, (8, 6 * Q))
        return carry

    lax.fori_loop(0, 36, small_turn, 0)

    def source_turn(number, carry):
        sx = number // 6
        sy = number % 6
        pieces = []
        for cx in range(2):
            for cy in range(2):
                for cz in range(2):
                    pieces.append(windows[sx + 2 * cx, sy + 2 * cy, pl.ds(8 * cz, 8), :])
        pieces.append(small[sx, sy])
        left = jnp.concatenate(pieces, axis=0)
        left_high = left.astype(jnp.bfloat16)
        left_low = (left - left_high.astype(jnp.float32)).astype(jnp.bfloat16)
        both = jnp.concatenate([left_high, left_low], axis=0)
        places = [(sx + 1 - cx, sy + 1 - cy) for cx in range(2) for cy in range(2)]
        right_high = jnp.concatenate([high[a, b] for a, b in places], axis=1)
        right_low = jnp.concatenate([low[a, b] for a, b in places], axis=1)
        first = jnp.dot(both, right_high, preferred_element_type=jnp.float32)
        second = jnp.dot(left_high, right_low, preferred_element_type=jnp.float32)
        total[...] += first[:80] + first[80:] + second
        return carry

    lax.fori_loop(0, 36, source_turn, 0)
    fitted = jnp.concatenate(
        [dot(total[:, 128 * pair : 128 * pair + 128], pair_fit[...]) for pair in range(4)], axis=1
    )

    def regroup(rows):
        return jnp.concatenate([rows[:, Q * c : Q * c + Q] for c in range(8)], axis=0)

    coarse = fitted[72:80] + dot(top_local[...], down[...])
    coarse = regroup(coarse[0:1])
    mid = regroup(fitted[64:72] + dot(coarse, down[...]))
    leaf = fitted[0:64] + dot(mid, down[...])
    for block in range(4):
        turned[...] = part[pl.ds(128 * block, 128), :].T
        own = leaf[:, 128 * block : 128 * block + 128]
        own = jnp.concatenate([own[:, :Q], own[:, Q:]], axis=0)
        local[...] = own.T * INV_FOUR_PI
        tx, ty, tz = turned[0:32], turned[32:64], turned[64:96]

        def point_turn(k, value):
            first = tx - spread[0, pl.ds(k, 1), :]
            second = ty - spread[1, pl.ds(k, 1), :]
            third = tz - spread[2, pl.ds(k, 1), :]
            inverse = lax.rsqrt(first * first + second * second + third * third)
            return value + inverse * local[pl.ds(k, 1), :]

        value = lax.fori_loop(0, Q, point_turn, jnp.zeros((32, 128), jnp.float32), unroll=4)
        out[pl.ds(128 * block, 128), :] = value.T


def run(kernel, outs, scratch, cost, limit, *args):
    return pl.pallas_call(
        kernel,
        out_shape=outs,
        scratch_shapes=[pltpu.VMEM(shape, jnp.float32) for shape in scratch],
        compiler_params=pltpu.CompilerParams(vmem_limit_bytes=limit),
        cost_estimate=pl.CostEstimate(flops=cost, bytes_accessed=1 << 20, transcendentals=0),
    )(*args)


def single(*shape):
    return jax.ShapeDtypeStruct(shape, jnp.float32)


def nested(cells):
    split = cells.reshape((2,) * 9 + cells.shape[3:])
    return split.transpose(2, 5, 8, 1, 4, 7, 0, 3, 6, 9).reshape(512, -1)


def plain(rows):
    split = rows.reshape((2,) * 9 + rows.shape[1:])
    return split.transpose(6, 3, 0, 7, 4, 1, 8, 5, 2, 9).reshape(8, 8, 8, -1)


def plain_mid(rows):
    split = rows.reshape((2,) * 6 + rows.shape[1:])
    return split.transpose(3, 0, 4, 1, 5, 2, 6).reshape(4, 4, 4, -1)


def extended(arrays, width):
    for axis, dim in (("gz", 2), ("gy", 1), ("gx", 0)):
        count = lax.axis_size(axis)
        heads = [lax.slice_in_dim(a, 0, width, axis=dim) for a in arrays]
        tails = [lax.slice_in_dim(a, a.shape[dim] - width, a.shape[dim], axis=dim) for a in arrays]
        forward = [(i, i + 1) for i in range(count - 1)]
        backward = [(i + 1, i) for i in range(count - 1)]

        def pack(parts):
            return jnp.concatenate([x.reshape(-1, x.shape[-1]) for x in parts], axis=0)

        def unpack(rows, parts):
            result, start = [], 0
            for x in parts:
                length = x.size // x.shape[-1]
                result.append(rows[start : start + length].reshape(x.shape))
                start += length
            return result

        before = unpack(lax.ppermute(pack(tails), axis, forward), tails)
        after = unpack(lax.ppermute(pack(heads), axis, backward), heads)
        arrays = [
            jnp.concatenate([b, a, c], axis=dim) for b, a, c in zip(before, arrays, after)
        ]
    return arrays


def far_local(top_row, points, fit):
    gathered = top_row
    index = jnp.zeros((1, 3), jnp.int32) + jnp.stack([lax.axis_index(axis) for axis in AXES])
    for place, axis in ((2, "gz"), (1, "gy"), (0, "gx")):
        count = lax.axis_size(axis)
        step, length = 1, gathered.shape[0]
        while step < count:
            take = min(step, count - step) * length
            ring = [(i, (i + step) % count) for i in range(count)]
            arrived = lax.ppermute(gathered[:take], axis, ring)
            from_index = index[:take, place] + (count - step)
            from_index = jnp.where(from_index >= count, from_index - count, from_index)
            moved = index[:take].at[:, place].set(from_index)
            gathered = jnp.concatenate([gathered, arrived], axis=0)
            index = jnp.concatenate([index, moved], axis=0)
            step *= 2
    own = jnp.stack([lax.axis_index(axis) for axis in AXES]).astype(jnp.float32)
    base = INNER * (points[:, :, None] - points[:, None, :])

    def block_term(total, number):
        rows = lax.dynamic_slice_in_dim(gathered, number * far_block, far_block, 0)
        boxes = lax.dynamic_slice_in_dim(index, number * far_block, far_block, 0)
        delta = own[None, :] - boxes.astype(jnp.float32)
        spread = jnp.max(jnp.abs(delta), axis=1)
        first = delta[:, 0, None, None] + base[0]
        second = delta[:, 1, None, None] + base[1]
        third = delta[:, 2, None, None] + base[2]
        square = first * first + second * second + third * third
        kernels = jnp.where(
            (spread >= 2.0)[:, None, None], INV_FOUR_PI / jnp.sqrt(square), 0.0
        )
        return (total + jnp.sum(kernels * rows[:, None, :], axis=(0, 2)), None)

    blocks = gathered.shape[0] // far_block
    check, _ = lax.scan(
        block_term, jnp.zeros((Q,), jnp.float32), jnp.arange(blocks, dtype=jnp.int32)
    )
    return jnp.dot(check[None, :], fit, precision=HIGHEST)


def per_device(particles, counts):
    points, fit, up, down, high, low, spread, pair_fit = constant_tables()
    slots = particles.shape[3] // 4
    present = jnp.arange(slots, dtype=jnp.int32) < counts[..., None]
    masked = jnp.concatenate(
        [particles[..., : 3 * slots], jnp.where(present, particles[..., 3 * slots :], 0.0)], axis=3
    )
    part = nested(masked)
    leaf, mid, coarse, top = run(
        upward_kernel,
        (single(512, Q), single(64, Q), single(8, Q), single(8, Q)),
        [(128, 128)],
        1 << 30,
        8 << 20,
        part,
        spread,
        np.ascontiguousarray(fit.T),
        up,
    )
    (padded_near,) = extended([masked], 1)
    near = jnp.concatenate(
        [
            run(
                functools.partial(near_kernel, start),
                single(128, 32),
                [(160, 128)],
                8 << 30,
                8 << 20,
                padded_near,
            )
            for start in (0, 2, 4, 6)
        ],
        axis=0,
    )
    top_local = far_local(top[0:1], points, fit)
    leaf_cells, mid_cells, coarse_cells = extended(
        [plain(leaf), plain_mid(mid), coarse.reshape(2, 2, 2, Q)], 2
    )
    far = run(
        downward_kernel,
        single(512, 32),
        [(80, 512), (128, 128), (Q, 128), (8, 8, 16, 6 * Q), (6, 6, 16, 6 * Q)],
        8 << 30,
        30 << 20,
        leaf_cells.reshape(144, 12 * Q),
        mid_cells.reshape(64, 8 * Q),
        coarse_cells.reshape(36, 6 * Q),
        high,
        low,
        pair_fit,
        down,
        jnp.broadcast_to(top_local, (8, Q)),
        part,
        spread,
    )
    near = near.reshape(8, 8, 8 * slots)
    return (plain(far).reshape(8, 8, 8 * slots) + near, near)


def solution(mesh):
    placed = (P("gx", "gy", "gz", None), P("gx", "gy", "gz"))
    return jax.shard_map(
        per_device,
        mesh=mesh,
        in_specs=placed,
        out_specs=(P("gx", "gy", "gz"), P("gx", "gy", "gz")),
        check_vma=False,
    )
```
